32 devices in a mesh: ctx: 2 (over y), section: 4 (over x, core), tp: 4 (over z).
Axes of the slice: x: 2, y: 2, z: 4, core: 2. Of those that a mesh axis runs over, the one named last changes fastest.
Arguments:
- queries: bfloat16 [256, 8192], P('ctx', ('section', 'tp')), may hold values from -140 to 140
- keys: bfloat16 [256, 1024], P('ctx', 'section'), may hold values from -6 to 6
- values: bfloat16 [256, 1024], P('ctx', 'section'), may hold values from -36 to 36
- out_grad: bfloat16 [256, 8192], P('ctx', ('section', 'tp')), may hold values from -6 to 6
- enc_weight: bfloat16 [8192, 65536], P(('section', 'tp'), 'ctx'), may hold values from -0.0625 to 0.0625
- enc_bias: float32 [65536], P(('ctx', 'section', 'tp')), may hold values from -3 to 3
- dec_weight: bfloat16 [65536, 8192], P('ctx', ('section', 'tp')), may hold values from -0.0625 to 0.0625
Outputs:
- query_grad: bfloat16 [256, 8192], P('ctx', ('section', 'tp'))
- gradient_keys: bfloat16 [256, 1024], P('ctx', 'section')
- gradient_values: bfloat16 [256, 1024], P('ctx', 'section')
- feature_scores: float32 [65536], P(('ctx', 'section', 'tp'))
The draws below stay inside these ranges and needn't reach their ends.
All inputs are finite; a program needn't handle non-finite values.
Results may differ from the reference program's by a relative error of at most 0.015.
Values may be sent and summed in bfloat16 or wider, within the bound.
No kernel may reach another device: no remote copies, remote signals or barrier semaphores. Data moves between devices by JAX's collectives and lax.ppermute only.
A program may use at most 256 MiB of HBM per device.

```python
import math
import jax
import jax.numpy as jnp
from jax import lax

QUERY_HEADS = 64
KEY_VALUE_HEADS = 8
HEAD_SIZE = 128
F = 65536
TQ = 128
SEQUENCE_TOKENS = 256
D_Z = 8192
N_CTX = 2


def paired_draws(key):
    query_key = jax.random.fold_in(key, 11)
    random_key_seed = jax.random.fold_in(key, 12)
    starting_keys = jnp.clip(jax.random.normal(random_key_seed, (SEQUENCE_TOKENS, KEY_VALUE_HEADS * HEAD_SIZE), jnp.float32), -6.0, 6.0)
    base_queries = jnp.clip(jax.random.normal(query_key, (SEQUENCE_TOKENS, QUERY_HEADS * HEAD_SIZE), jnp.float32), -6.0, 6.0)
    return (base_queries, starting_keys)


def draw_queries(key, part):
    return paired_draws(key)[0].astype(jnp.bfloat16)


def draw_keys(key, part):
    return paired_draws(key)[1].astype(jnp.bfloat16)


def draw_values(key, part):
    noise_level = jnp.clip(jax.random.normal(jax.random.fold_in(key, 13), (SEQUENCE_TOKENS, KEY_VALUE_HEADS * HEAD_SIZE), jnp.float32), -4.0, 4.0)
    head_of_column = (jnp.arange(KEY_VALUE_HEADS * HEAD_SIZE, dtype=jnp.int32) // HEAD_SIZE).astype(jnp.float32)
    spread_factor = 2.0
    growth_factor = 1.0 + spread_factor * head_of_column / max(KEY_VALUE_HEADS - 1, 1)
    return (noise_level * growth_factor[None, :]).astype(jnp.bfloat16)


def block_levels(stream_key, shape, shards, smallest, top_value):
    loudness, own = 1.0, jax.random.fold_in(stream_key, 6)
    for dim, blocks in shards:
        steps = jnp.exp(jax.random.uniform(jax.random.fold_in(own, dim), (blocks,), jnp.float32, smallest / len(shards), top_value / len(shards)))
        loudness = loudness * jnp.repeat(steps, shape[dim] // blocks).reshape([-1 if axis == dim else 1 for axis in range(len(shape))])
    return loudness


def noise(stream_key, shape, deviation, bound, split=(), held_as=jnp.bfloat16):
    drawn = deviation * jax.random.normal(stream_key, shape, jnp.float32)
    if split:
        drawn = drawn * block_levels(stream_key, shape, split, -0.22, 0.18)
    return jnp.clip(drawn, -bound, bound).astype(held_as)


def setup_inputs(seed: int = 0) -> dict:
    seeds = jax.random.split(jax.random.key(seed), 8)
    queries = draw_queries(jax.random.fold_in(seeds[7], 71), 0)
    keys = draw_keys(jax.random.fold_in(seeds[7], 71), 0)
    values = draw_values(jax.random.fold_in(seeds[7], 71), 0)
    out_grad = noise(seeds[3], (SEQUENCE_TOKENS, D_Z), 1.0, 6.0, ((0, 2), (1, 16)))
    enc_weight = noise(seeds[4], (D_Z, F), D_Z ** -0.5, 0.0625, ((0, 16), (1, 2)))
    enc_bias = noise(seeds[5], (F,), 0.5, 3.0, ((0, 32),), jnp.float32)
    dec_weight = noise(seeds[6], (F, D_Z), D_Z ** -0.5, 0.0625, ((0, 2), (1, 16)))
    return {"queries": queries, "keys": keys, "values": values, "out_grad": out_grad, "enc_weight": enc_weight, "enc_bias": enc_bias, "dec_weight": dec_weight}


def row_positions(sequence_length):
    half = TQ // 2
    rows = jnp.arange(sequence_length, dtype=jnp.int32)
    half_block = rows // half
    owner = half_block // 2
    block = jnp.where(half_block % 2 == 0, owner, 2 * N_CTX - 1 - owner)
    return (block * half + rows % half).astype(jnp.int32)

def reference(queries, keys, values, out_grad, enc_weight, enc_bias, dec_weight):
    sequence_length = queries.shape[0]
    group_width = QUERY_HEADS // KEY_VALUE_HEADS
    score_scale = 1.0 / math.sqrt(HEAD_SIZE)
    positions = row_positions(sequence_length)
    causal = positions[:, None] >= positions[None, :]

    def one_head(head_index):
        kv_index = head_index // group_width
        query_head = lax.dynamic_slice_in_dim(queries, (head_index * HEAD_SIZE).astype(jnp.int32), HEAD_SIZE, 1)
        grad_head = lax.dynamic_slice_in_dim(out_grad, (head_index * HEAD_SIZE).astype(jnp.int32), HEAD_SIZE, 1)
        key_head = lax.dynamic_slice_in_dim(keys, (kv_index * HEAD_SIZE).astype(jnp.int32), HEAD_SIZE, 1)
        value_head = lax.dynamic_slice_in_dim(values, (kv_index * HEAD_SIZE).astype(jnp.int32), HEAD_SIZE, 1)
        logits = jnp.dot(query_head, key_head.T, preferred_element_type=jnp.float32) * score_scale
        log_total = jax.nn.logsumexp(jnp.where(causal, logits, -jnp.inf), axis=1)
        weights = jnp.where(causal, jnp.exp(logits - log_total[:, None]), 0.0)
        head_out = jnp.dot(weights, value_head.astype(jnp.float32), precision=lax.Precision.HIGHEST).astype(jnp.bfloat16)
        row_dots = lax.optimization_barrier(jnp.sum(grad_head.astype(jnp.float32) * head_out.astype(jnp.float32), axis=1))
        weights_half = weights.astype(jnp.bfloat16)
        value_part = jnp.dot(weights_half.T, grad_head, preferred_element_type=jnp.float32)
        weight_grad = jnp.dot(grad_head, value_head.T, preferred_element_type=jnp.float32)
        logit_half = (weights * (weight_grad - row_dots[:, None])).astype(jnp.bfloat16)
        query_part = (jnp.dot(logit_half, key_head, preferred_element_type=jnp.float32) * score_scale).astype(jnp.bfloat16)
        key_part = jnp.dot(logit_half.T, query_head, preferred_element_type=jnp.float32) * score_scale
        return (head_out, query_part, key_part, value_part)
    head_outs, query_parts, key_pieces, value_pieces = lax.map(one_head, jnp.arange(QUERY_HEADS, dtype=jnp.int32))
    attn_out = jnp.transpose(head_outs, (1, 0, 2)).reshape(sequence_length, QUERY_HEADS * HEAD_SIZE)
    query_grad = jnp.transpose(query_parts, (1, 0, 2)).reshape(sequence_length, QUERY_HEADS * HEAD_SIZE)
    summed_keys = lax.optimization_barrier(jnp.sum(key_pieces.reshape(KEY_VALUE_HEADS, group_width, sequence_length, HEAD_SIZE), axis=1))
    summed_values = lax.optimization_barrier(jnp.sum(value_pieces.reshape(KEY_VALUE_HEADS, group_width, sequence_length, HEAD_SIZE), axis=1))
    gradient_keys = jnp.transpose(summed_keys, (1, 0, 2)).reshape(sequence_length, KEY_VALUE_HEADS * HEAD_SIZE).astype(jnp.bfloat16)
    gradient_values = jnp.transpose(summed_values, (1, 0, 2)).reshape(sequence_length, KEY_VALUE_HEADS * HEAD_SIZE).astype(jnp.bfloat16)
    last_out = attn_out[sequence_length - TQ:]
    last_grad = out_grad[sequence_length - TQ:]
    wide_out = last_out.astype(jnp.float32)
    rms = jnp.sqrt(lax.optimization_barrier(jnp.sum(wide_out * wide_out, axis=1)) / D_Z + 1e-06)
    active = jnp.maximum(jnp.dot(last_out, enc_weight, preferred_element_type=jnp.float32) / rms[:, None] + enc_bias[None, :], 0.0)
    attrib = jnp.dot(last_grad, dec_weight.T, preferred_element_type=jnp.float32)
    feature_scores = lax.optimization_barrier(jnp.sum(active * attrib, axis=0))
    return (query_grad, gradient_keys, gradient_values, feature_scores)
```

```python
import functools
import math

import jax
import jax.numpy as jnp
from jax import lax
from jax.experimental import pallas as pl
from jax.experimental.pallas import tpu as pltpu
from jax.sharding import PartitionSpec as P

QUERY_HEADS = 64
KEY_VALUE_HEADS = 8
HEAD_SIZE = 128
D_Z = 8192

SCHEDULE = (
    ("dec", 0, 384, (0, 1, 3, 5, 7)),
    ("dec", 384, 640, (0, 2, 4, 6, 8)),
    ("dec", 1024, 1024, (1, 3, 5, 7, 9)),
    ("enc", 1280, 768, (2, 4, 6, 8, 10)),
    ("enc", 640, 640, (3, 5, 7, 9, 10)),
    ("enc", 256, 384, (4, 6, 8, 10, 11)),
    ("enc", 0, 256, (5, 7, 9, 10, 11)),
)
SHORT_SCHEDULE = (("dec", 0, 1, (0, 2, 4, 6, 8)), ("enc", 0, 1, (1, 3, 5, 7, 9)))
COST = 100
ATTENTION_STEP = 0
FIRST_SQUARES = 4
FIRST_TERMS = 3


def shifted(value, axis, steps):
    count = lax.axis_size(axis)
    return lax.ppermute(value, axis, [(i, (i + steps) % count) for i in range(count)])


def swapped(value, axis, mask):
    count = lax.axis_size(axis)
    return lax.ppermute(value, axis, [(i, i ^ mask) for i in range(count)])


def from_last(value, axis):
    count = lax.axis_size(axis)
    rank = count - 1 - lax.axis_index(axis)
    reach = 1
    while reach < count:
        pairs = [
            (count - 1 - i, count - 1 - i - reach) for i in range(reach) if i + reach < count
        ]
        moved = lax.ppermute(value, axis, pairs)
        value = jnp.where((rank >= reach) & (rank < 2 * reach), moved, value)
        reach *= 2
    return value


def attention_kernel(cycle_size, queries, out_grad, *refs):
    pairs, (attn, query_grad, *terms) = refs[:cycle_size], refs[cycle_size:]
    rows, columns = queries.shape
    half = rows // 2
    scale = 1.0 / math.sqrt(HEAD_SIZE)
    me = lax.axis_index("ctx")

    def positions(device, axis):
        local = lax.broadcasted_iota(jnp.int32, (rows, rows), axis)
        late = (2 * cycle_size - 1 - device) * half + local - half
        return jnp.where(local >= half, late, device * half + local)

    mine = positions(me, 0)
    causal = jnp.concatenate(
        [
            (mine - positions(lax.rem(me + turn, cycle_size), 1)).astype(jnp.float32)
            for turn in range(cycle_size)
        ],
        axis=1,
    ) >= 0.0
    keys = jnp.concatenate([ref[0] for ref in pairs], axis=0)
    values = jnp.concatenate([ref[1] for ref in pairs], axis=0)
    key_term = value_term = 0.0

    def dot(left, right, left_dim, right_dim):
        return lax.dot_general(
            left, right, (((left_dim,), (right_dim,)), ((), ())),
            preferred_element_type=jnp.float32,
        )

    for first in range(0, columns, HEAD_SIZE):
        head = slice(first, first + HEAD_SIZE)
        query, grad = queries[:, head], out_grad[:, head]
        logits = jnp.where(causal, dot(query, keys, 1, 1) * scale, -1e30)
        raised = jnp.where(causal, jnp.exp(logits - jnp.max(logits, axis=1, keepdims=True)), 0.0)
        weights = raised / jnp.sum(raised, axis=1, keepdims=True)
        high = weights.astype(jnp.bfloat16)
        low = (weights - high.astype(jnp.float32)).astype(jnp.bfloat16)
        out = (dot(high, values, 1, 0) + dot(low, values, 1, 0)).astype(jnp.bfloat16)
        attn[:, head] = out
        row_dots = jnp.sum(
            grad.astype(jnp.float32) * out.astype(jnp.float32), axis=1, keepdims=True
        )
        value_term += dot(high, grad, 0, 0)
        logit_half = (weights * (dot(grad, values, 1, 1) - row_dots)).astype(jnp.bfloat16)
        query_grad[:, head] = (dot(logit_half, keys, 1, 0) * scale).astype(jnp.bfloat16)
        key_term += dot(logit_half, query, 0, 0)
    for turn, ref in enumerate(terms):
        block = slice(turn * rows, (turn + 1) * rows)
        ref[0] = key_term[block] * scale
        ref[1] = value_term[block]


def relative_blocks(order, stage, size):
    done = sum(order[:stage])
    bit = order[stage] if stage < len(order) else 0
    return [r for r in range(size) if not r & done and (r & bit or r == bit)]


class Chunk:
    def __init__(self, kind, offset, width, steps, order):
        self.kind, self.offset, self.width, self.order = kind, offset, width, order
        self.steps = steps
        self.received = []
        self.result = None


def step_kernel(plan, size, latents, tp, *refs):
    refs = list(refs)
    take = lambda count: [refs.pop(0) for _ in range(count)]
    sources = {kind: take(2) for kind in plan["kinds"]}
    jobs = plan["jobs"]
    incoming = [take(stage) for _, stage in jobs]
    extras = [take(2 + len(pieces)) if pieces else () for pieces in plan["pieces"]]
    outs = take(len(jobs))
    weight_bufs, sum_bufs, out_bufs = [], [], []
    for _, stage in jobs:
        weight_bufs.append(take(1)[0])
        sum_bufs.append(take(stage))
        out_bufs.append(take(1)[0])
    sems = take(1)[0]
    me = lax.axis_index("section") * tp + lax.axis_index("tp")
    used = 0

    def copy(source, target):
        nonlocal used
        used += 1
        return pltpu.make_async_copy(source, target, sems.at[used - 1])

    arrivals = []
    for number, (chunk, stage) in enumerate(jobs):
        blocks = relative_blocks(chunk.order, stage, size)
        weight = sources[chunk.kind][1]
        for index, r in enumerate(blocks):
            first = pl.multiple_of((me ^ r) * latents + chunk.offset, 128)
            if chunk.kind == "dec":
                piece = weight.at[pl.ds(first, chunk.width), :]
            else:
                piece = weight.at[:, pl.ds(first, chunk.width)]
            wanted = [copy(piece, weight_bufs[number].at[index])]
            for earlier in range(stage):
                sent = relative_blocks(chunk.order, earlier, size)
                place = sent.index(r ^ chunk.order[earlier])
                wanted.append(
                    copy(incoming[number][earlier].at[place], sum_bufs[number][earlier].at[index])
                )
            for item in wanted:
                item.start()
            arrivals.append(wanted)
    leaving = []
    for number, (chunk, stage) in enumerate(jobs):
        act = sources[chunk.kind][0]
        for index in range(len(relative_blocks(chunk.order, stage, size))):
            for item in arrivals.pop(0):
                item.wait()
            total = lax.dot_general(
                act[...],
                weight_bufs[number][index],
                (((1,), (1 if chunk.kind == "dec" else 0,)), ((), ())),
                preferred_element_type=jnp.float32,
            )
            for buf in sum_bufs[number]:
                total = total + buf[index].astype(jnp.float32)
            if plan["pieces"][number]:
                inverse, bias, *attribs = extras[number]
                active = jnp.maximum(total * inverse[:, :1] + bias[...], 0.0)
                attrib = [
                    ref[0, :, first:last]
                    for ref, (first, last) in zip(attribs, plan["pieces"][number])
                ]
                attrib = attrib[0] if len(attrib) == 1 else jnp.concatenate(attrib, axis=1)
                total = jnp.sum(active * attrib, axis=0, keepdims=True)
            out_bufs[number][index] = total.astype(out_bufs[number].dtype)
            item = copy(out_bufs[number].at[index], outs[number].at[index])
            item.start()
            leaving.append(item)
    for item in leaving:
        item.wait()


def run_step(jobs, acts, weights, size, latents, tp, finish):
    kinds = [kind for kind in ("dec", "enc") if any(c.kind == kind for c, _ in jobs)]
    rows, inner = acts[kinds[0]].shape
    operands, specs = [], []
    anywhere = pl.BlockSpec(memory_space=pltpu.HBM)
    vmem = pl.BlockSpec(memory_space=pltpu.VMEM)
    for kind in kinds:
        operands += [acts[kind], weights[kind]]
        specs += [vmem, anywhere]
    for chunk, stage in jobs:
        operands += chunk.received[:stage]
        specs += [anywhere] * stage
    outs, scratch, copies, flops, moved = [], [], 0, 0, 0
    pieces = []
    for chunk, stage in jobs:
        last = stage == len(chunk.order)
        pieces.append(())
        if last and chunk.kind == "enc":
            values, pieces[-1] = finish(chunk)
            operands += values
            specs += [vmem] * len(values)
        count = len(relative_blocks(chunk.order, stage, size))
        shape = (count, rows, chunk.width)
        if last:
            dtype = jnp.float32
            if chunk.kind == "enc":
                shape = (1, 1, chunk.width)
        else:
            dtype = jnp.bfloat16
        outs.append(jax.ShapeDtypeStruct(shape, dtype))
        side = (chunk.width, inner) if chunk.kind == "dec" else (inner, chunk.width)
        scratch.append(pltpu.VMEM((count, *side), jnp.bfloat16))
        scratch += [pltpu.VMEM((count, rows, chunk.width), jnp.bfloat16)] * stage
        scratch.append(pltpu.VMEM(shape, dtype))
        copies += count * (stage + 2)
        flops += 2 * count * rows * inner * chunk.width
        moved += 2 * count * chunk.width * (inner + (stage + 1) * rows)
    results = pl.pallas_call(
        functools.partial(step_kernel, {"kinds": kinds, "jobs": jobs, "pieces": pieces}, size, latents, tp),
        out_shape=outs,
        in_specs=specs,
        out_specs=[anywhere] * len(outs),
        scratch_shapes=[*scratch, pltpu.SemaphoreType.DMA((copies,))],
        compiler_params=pltpu.CompilerParams(vmem_limit_bytes=24 * 2**20),
        cost_estimate=pl.CostEstimate(
            flops=int(COST * flops), bytes_accessed=int(COST * moved), transcendentals=0
        ),
    )(*operands)
    for kind in acts:
        acts[kind], _ = lax.optimization_barrier((acts[kind], results[0]))
    for (chunk, stage), value in zip(jobs, results):
        chunk.latest = value
        if stage == len(chunk.order):
            chunk.result = value
        elif chunk.order[stage] >= tp:
            chunk.received.append(swapped(value, "section", chunk.order[stage] // tp))
        else:
            chunk.received.append(swapped(value, "tp", chunk.order[stage]))


def body(queries, keys, values, out_grad, enc_weight, enc_bias, dec_weight):
    row_count = queries.shape[0]
    heads_here = queries.shape[1] // HEAD_SIZE
    kv_here = keys.shape[1] // HEAD_SIZE
    group_width = QUERY_HEADS // KEY_VALUE_HEADS
    cycle_size = lax.axis_size("ctx")
    section_size, tp_size = lax.axis_size("section"), lax.axis_size("tp")
    tp_index = lax.axis_index("tp")
    local_kv = tp_index * heads_here // group_width
    group = (
        lax.axis_index("section") * tp_size + tp_index,
        section_size * tp_size,
        tp_size,
    )
    core, across, near, far = tp_size, 2 * tp_size, 1, 2
    order = (core, across, near, far)

    scored_grad = from_last(out_grad, "ctx")
    latents = enc_weight.shape[1] // group[1]
    weights = {"dec": dec_weight, "enc": enc_weight}
    full = max(first + width for _, first, width, _ in SCHEDULE)
    schedule, unit = (SHORT_SCHEDULE, latents) if latents % full else (SCHEDULE, latents // full)
    chunks = [
        Chunk(kind, first * unit, width * unit, times, order)
        for kind, first, width, times in schedule
    ]
    steps = [
        [(chunk, chunk.steps.index(step)) for chunk in chunks if step in chunk.steps]
        for step in range(1 + max(chunk.steps[-1] for chunk in chunks))
    ]
    acts = {"dec": scored_grad}
    early = next(step for step, jobs in enumerate(steps) if any(c.kind == "enc" for c, _ in jobs))
    for step in range(early):
        run_step(steps[step], acts, weights, group[1], latents, tp_size, None)
        if step == ATTENTION_STEP:
            queries, _ = lax.optimization_barrier((queries, acts["dec"]))

    pair = jnp.stack(
        [
            lax.dynamic_slice_in_dim(keys, local_kv * HEAD_SIZE, HEAD_SIZE, 1),
            lax.dynamic_slice_in_dim(values, local_kv * HEAD_SIZE, HEAD_SIZE, 1),
        ]
    )
    pairs = [pair] + [shifted(pair, "ctx", -turn) for turn in range(1, cycle_size)]
    attn_flat, query_grad, *terms = pl.pallas_call(
        functools.partial(attention_kernel, cycle_size),
        out_shape=[
            jax.ShapeDtypeStruct(queries.shape, jnp.bfloat16),
            jax.ShapeDtypeStruct(queries.shape, jnp.bfloat16),
            *[jax.ShapeDtypeStruct(pair.shape, jnp.float32)] * cycle_size,
        ],
        compiler_params=pltpu.CompilerParams(vmem_limit_bytes=32 * 2**20),
    )(queries, out_grad, *pairs)
    scored_out = from_last(attn_flat, "ctx")
    wide_out = scored_out.astype(jnp.float32)
    squares = jnp.sum(wide_out * wide_out, axis=1)
    acts["enc"], _ = lax.optimization_barrier((scored_out, acts["dec"]))

    def add_squares(axis, mask, token):
        nonlocal squares
        other = swapped(squares, axis, mask)
        squares, _ = lax.optimization_barrier((squares, token))
        squares = squares + other

    def gather_blocks(token):
        nonlocal summed
        others = [shifted(terms[turn], "ctx", turn) for turn in range(1, cycle_size)]
        summed, _ = lax.optimization_barrier((terms[0], token))
        for other in others:
            summed = summed + other

    def add_heads(mask, token):
        nonlocal summed
        other = swapped(summed, "tp", mask)
        summed, _ = lax.optimization_barrier((summed, token))
        summed = summed + other

    def gather_heads(token):
        nonlocal summed
        half = summed.astype(jnp.bfloat16)
        others = [swapped(half, "tp", share * step) for step in range(1, kv_here)]
        half, _ = lax.optimization_barrier((half, token))
        slots, columns = [half, *others], []
        for column in range(kv_here):
            value = slots[0]
            for step in range(1, kv_here):
                value = jnp.where((local_kv ^ step) == column, slots[step], value)
            columns.append(value)
        summed = jnp.concatenate(columns, axis=2)

    summed = terms[0]
    share = group_width // heads_here
    bits = lambda count: [1 << i for i in range((count - 1).bit_length())]
    tasks = {}
    square_tasks = [functools.partial(add_squares, "section", m) for m in bits(section_size)]
    square_tasks += [functools.partial(add_squares, "tp", m) for m in bits(tp_size)]
    term_tasks = [gather_blocks]
    term_tasks += [functools.partial(add_heads, mask) for mask in bits(share)]
    term_tasks += [gather_heads]
    for first, items in ((FIRST_SQUARES, square_tasks), (FIRST_TERMS, term_tasks)):
        for number, item in enumerate(items):
            tasks.setdefault(first + number, []).append(item)

    bias = enc_bias.reshape(1, latents)

    def finish(chunk):
        end = chunk.offset + chunk.width
        inverse = jnp.broadcast_to(
            lax.rsqrt(squares / D_Z + 1e-06)[:, None], (row_count, HEAD_SIZE)
        )
        values, pieces = [inverse, lax.slice_in_dim(bias, chunk.offset, end, axis=1)], []
        for other in chunks:
            first, last = max(other.offset, chunk.offset), min(other.offset + other.width, end)
            if other.kind == "dec" and first < last:
                values.append(other.result)
                pieces.append((first - other.offset, last - other.offset))
        return values, pieces

    for step, jobs in enumerate(steps[early:], early):
        run_step(jobs, acts, weights, group[1], latents, tp_size, finish)
        for task in tasks.get(step, ()):
            task(acts["enc"])
        if step in tasks:
            acts["enc"], _, _ = lax.optimization_barrier((acts["enc"], squares, summed))
    scores = sorted((c for c in chunks if c.kind == "enc"), key=lambda c: c.offset)
    feature_scores = jnp.concatenate([c.result[0] for c in scores], axis=1).reshape(latents)
    return (query_grad, summed[0], summed[1], feature_scores)


def solution(mesh):
    placed = (
        P("ctx", ("section", "tp")),
        P("ctx", "section"),
        P("ctx", "section"),
        P("ctx", ("section", "tp")),
        P(("section", "tp"), "ctx"),
        P(("ctx", "section", "tp")),
        P("ctx", ("section", "tp")),
    )
    return jax.shard_map(
        body,
        mesh=mesh,
        in_specs=placed,
        out_specs=(
            P("ctx", ("section", "tp")),
            P("ctx", "section"),
            P("ctx", "section"),
            P(("ctx", "section", "tp")),
        ),
        check_vma=False,
    )
```

```python
import functools
import math

import jax
import jax.numpy as jnp
from jax import lax
from jax.experimental import pallas as pl
from jax.experimental.pallas import tpu as pltpu
from jax.sharding import PartitionSpec as P

QUERY_HEADS = 64
KEY_VALUE_HEADS = 8
HEAD_SIZE = 128
D_Z = 8192

SCHEDULE = (
    ("dec", 0, 512, (0, 1, 3, 5, 7), False),
    ("dec", 512, 512, (0, 2, 4, 6, 8), True),
    ("dec", 1024, 1024, (1, 3, 5, 7, 9), False),
    ("enc", 1280, 768, (2, 4, 6, 8, 10), False),
    ("enc", 768, 512, (3, 5, 7, 9, 10), False),
    ("enc", 256, 512, (4, 6, 8, 10, 11), False),
    ("enc", 0, 256, (5, 7, 9, 10, 11), False),
)
SHORT_SCHEDULE = (
    ("dec", 0, 1, (0, 2, 4, 6, 8), False),
    ("enc", 0, 1, (1, 3, 5, 7, 9), False),
)
COST = 100
AHEAD = 8
TOGETHER = 2048
FIRST_SQUARES = 4
FIRST_TERMS = 3


def shifted(value, axis, steps):
    count = lax.axis_size(axis)
    return lax.ppermute(value, axis, [(i, (i + steps) % count) for i in range(count)])


def swapped(value, axis, mask):
    count = lax.axis_size(axis)
    return lax.ppermute(value, axis, [(i, i ^ mask) for i in range(count)])


def from_last(value, axis, tokens=()):
    count = lax.axis_size(axis)
    rank = count - 1 - lax.axis_index(axis)
    reach = 1
    while reach < count:
        pairs = [
            (count - 1 - i, count - 1 - i - reach) for i in range(reach) if i + reach < count
        ]
        moved = lax.ppermute(value, axis, pairs)
        value, *_ = lax.optimization_barrier((value, *tokens))
        tokens = ()
        value = jnp.where((rank >= reach) & (rank < 2 * reach), moved, value)
        reach *= 2
    return value


def attention_kernel(cycle_size, queries, out_grad, *refs):
    pairs, (attn, query_grad, *terms) = refs[:cycle_size], refs[cycle_size:]
    rows, columns = queries.shape
    half = rows // 2
    scale = 1.0 / math.sqrt(HEAD_SIZE)
    me = lax.axis_index("ctx")

    def positions(device, axis):
        local = lax.broadcasted_iota(jnp.int32, (rows, rows), axis)
        late = (2 * cycle_size - 1 - device) * half + local - half
        return jnp.where(local >= half, late, device * half + local)

    mine = positions(me, 0)
    causal = jnp.concatenate(
        [
            (mine - positions(lax.rem(me + turn, cycle_size), 1)).astype(jnp.float32)
            for turn in range(cycle_size)
        ],
        axis=1,
    ) >= 0.0
    keys = jnp.concatenate([ref[0] for ref in pairs], axis=0)
    values = jnp.concatenate([ref[1] for ref in pairs], axis=0)
    key_term = value_term = 0.0

    def dot(left, right, left_dim, right_dim):
        return lax.dot_general(
            left, right, (((left_dim,), (right_dim,)), ((), ())),
            preferred_element_type=jnp.float32,
        )

    for first in range(0, columns, HEAD_SIZE):
        head = slice(first, first + HEAD_SIZE)
        query, grad = queries[:, head], out_grad[:, head]
        logits = jnp.where(causal, dot(query, keys, 1, 1) * scale, -1e30)
        raised = jnp.where(causal, jnp.exp(logits - jnp.max(logits, axis=1, keepdims=True)), 0.0)
        weights = raised / jnp.sum(raised, axis=1, keepdims=True)
        high = weights.astype(jnp.bfloat16)
        low = (weights - high.astype(jnp.float32)).astype(jnp.bfloat16)
        out = (dot(high, values, 1, 0) + dot(low, values, 1, 0)).astype(jnp.bfloat16)
        attn[:, head] = out
        row_dots = jnp.sum(
            grad.astype(jnp.float32) * out.astype(jnp.float32), axis=1, keepdims=True
        )
        value_term += dot(high, grad, 0, 0)
        logit_half = (weights * (dot(grad, values, 1, 1) - row_dots)).astype(jnp.bfloat16)
        query_grad[:, head] = (dot(logit_half, keys, 1, 0) * scale).astype(jnp.bfloat16)
        key_term += dot(logit_half, query, 0, 0)
    for turn, ref in enumerate(terms):
        block = slice(turn * rows, (turn + 1) * rows)
        ref[0] = key_term[block] * scale
        ref[1] = value_term[block]


def relative_blocks(order, stage, size):
    done = sum(order[:stage])
    bit = order[stage] if stage < len(order) else 0
    return [r for r in range(size) if not r & done and (r & bit or r == bit)]


class Chunk:
    def __init__(self, kind, offset, width, steps, order):
        self.kind, self.offset, self.width, self.order = kind, offset, width, order
        self.steps = steps
        self.received = []
        self.result = None


def step_kernel(plan, size, latents, tp, *refs):
    refs = list(refs)
    take = lambda count: [refs.pop(0) for _ in range(count)]
    kinds, jobs, pieces = plan["kinds"], plan["jobs"], plan["pieces"]
    sources = {kind: take(2) for kind in kinds}
    incoming = [take(stage) for _, stage in jobs]
    extras = [take(2 + len(piece)) if piece else () for piece in pieces]
    outs = take(len(jobs))
    acts = {kind: take(1)[0] for kind in kinds}
    weight_bufs, sum_bufs, out_bufs, extra_bufs = [], [], [], []
    for (_, stage), piece in zip(jobs, pieces):
        weight_bufs.append(take(1)[0])
        sum_bufs.append(take(stage))
        out_bufs.append(take(1)[0])
        extra_bufs.append(take(3) if piece else ())
    sems = take(1)[0]
    me = lax.axis_index("section") * tp + lax.axis_index("tp")
    used = 0

    def copy(source, target):
        nonlocal used
        used += 1
        return pltpu.make_async_copy(source, target, sems.at[used - 1])

    arrivals, seen = [], set()
    for number, (chunk, stage) in enumerate(jobs):
        blocks = relative_blocks(chunk.order, stage, size)
        weight = sources[chunk.kind][1]
        for index, r in enumerate(blocks):
            first = pl.multiple_of((me ^ r) * latents + chunk.offset, 128)
            if chunk.kind == "dec":
                piece = weight.at[pl.ds(first, chunk.width), :]
            else:
                piece = weight.at[:, pl.ds(first, chunk.width)]
            wanted = [copy(piece, weight_bufs[number].at[index])]
            if chunk.kind not in seen:
                seen.add(chunk.kind)
                wanted.insert(0, copy(sources[chunk.kind][0], acts[chunk.kind]))
            for earlier in range(stage):
                for place, to, count in runs(chunk.order, earlier, stage, size):
                    if to == index:
                        source = incoming[number][earlier].at[pl.ds(place, count)]
                        target = sum_bufs[number][earlier].at[pl.ds(to, count)]
                        wanted.append(copy(source, target))
            if pieces[number]:
                inverse, bias, *attribs = extras[number]
                inverse_buf, bias_buf, attrib_buf = extra_bufs[number]
                wanted.append(copy(inverse, inverse_buf))
                wanted.append(copy(bias.at[:, pl.ds(chunk.offset, chunk.width)], bias_buf))
                place = 0
                for ref, (first, last) in zip(attribs, pieces[number]):
                    source = ref.at[0, :, pl.ds(first, last - first)]
                    wanted.append(copy(source, attrib_buf.at[:, pl.ds(place, last - first)]))
                    place += last - first
            arrivals.append(wanted)
    for item in sum(arrivals[:AHEAD], []):
        item.start()
    leaving, current = [], 0
    for number, (chunk, stage) in enumerate(jobs):
        act = acts[chunk.kind]
        count, sent = len(relative_blocks(chunk.order, stage, size)), 0
        for index in range(count):
            for item in arrivals[current]:
                item.wait()
            for item in sum(arrivals[current + AHEAD : current + AHEAD + 1], []):
                item.start()
            current += 1
            total = lax.dot_general(
                act[...],
                weight_bufs[number][index],
                (((1,), (1 if chunk.kind == "dec" else 0,)), ((), ())),
                preferred_element_type=jnp.float32,
            )
            for buf in sum_bufs[number]:
                total = total + buf[index].astype(jnp.float32)
            if pieces[number]:
                inverse_buf, bias_buf, attrib_buf = extra_bufs[number]
                active = jnp.maximum(total * inverse_buf[:, :1] + bias_buf[...], 0.0)
                total = jnp.sum(active * attrib_buf[...], axis=0, keepdims=True)
            out_bufs[number][index] = total.astype(out_bufs[number].dtype)
            if index + 1 == count or (index + 1 - sent) * chunk.width >= TOGETHER:
                part = pl.ds(sent, index + 1 - sent)
                item = copy(out_bufs[number].at[part], outs[number].at[part])
                item.start()
                leaving.append(item)
                sent = index + 1
    for item in leaving:
        item.wait()


def runs(order, earlier, stage, size):
    sent = relative_blocks(order, earlier, size)
    found = []
    for index, r in enumerate(relative_blocks(order, stage, size)):
        place = sent.index(r ^ order[earlier])
        if found and found[-1][0] + found[-1][2] == place:
            found[-1][2] += 1
        else:
            found.append([place, index, 1])
    return found


def run_step(jobs, acts, weights, size, latents, tp, finish):
    kinds = [kind for kind in ("dec", "enc") if any(c.kind == kind for c, _ in jobs)]
    rows, inner = acts[kinds[0]].shape
    operands = []
    anywhere = pl.BlockSpec(memory_space=pltpu.HBM)
    for kind in kinds:
        operands += [acts[kind], weights[kind]]
    for chunk, stage in jobs:
        operands += chunk.received[:stage]
    scratch = [pltpu.VMEM((rows, inner), jnp.bfloat16)] * len(kinds)
    outs, pieces, copies, flops, moved = [], [], len(kinds), 0, 0
    for chunk, stage in jobs:
        last = stage == len(chunk.order)
        count = len(relative_blocks(chunk.order, stage, size))
        shape = (count, rows, chunk.width)
        dtype = jnp.float32 if last else jnp.bfloat16
        pieces.append(())
        side = (chunk.width, inner) if chunk.kind == "dec" else (inner, chunk.width)
        scratch.append(pltpu.VMEM((count, *side), jnp.bfloat16))
        scratch += [pltpu.VMEM(shape, jnp.bfloat16)] * stage
        if last and chunk.kind == "enc":
            values, pieces[-1] = finish(chunk)
            operands += values
            copies += len(values)
            shape = (1, 1, chunk.width)
        scratch.append(pltpu.VMEM(shape, dtype))
        if pieces[-1]:
            scratch += [
                pltpu.VMEM((rows, HEAD_SIZE), jnp.float32),
                pltpu.VMEM((1, chunk.width), jnp.float32),
                pltpu.VMEM((rows, chunk.width), jnp.float32),
            ]
        outs.append(jax.ShapeDtypeStruct(shape, dtype))
        copies += count * (stage + 2)
        flops += 2 * count * rows * inner * chunk.width
        moved += 2 * count * chunk.width * (inner + (stage + 1) * rows)
    results = pl.pallas_call(
        functools.partial(
            step_kernel, {"kinds": kinds, "jobs": jobs, "pieces": pieces}, size, latents, tp
        ),
        out_shape=outs,
        in_specs=[anywhere] * len(operands),
        out_specs=[anywhere] * len(outs),
        scratch_shapes=[*scratch, pltpu.SemaphoreType.DMA((copies,))],
        compiler_params=pltpu.CompilerParams(vmem_limit_bytes=32 * 2**20),
        cost_estimate=pl.CostEstimate(
            flops=int(COST * flops), bytes_accessed=int(COST * moved), transcendentals=0
        ),
    )(*operands)
    for kind in acts:
        acts[kind], _ = lax.optimization_barrier((acts[kind], results[0]))
    for (chunk, stage), value in zip(jobs, results):
        chunk.latest = value
        if stage == len(chunk.order):
            chunk.result = value
        elif chunk.order[stage] >= tp:
            chunk.received.append(swapped(value, "section", chunk.order[stage] // tp))
        else:
            chunk.received.append(swapped(value, "tp", chunk.order[stage]))


def body(queries, keys, values, out_grad, enc_weight, enc_bias, dec_weight):
    row_count = queries.shape[0]
    heads_here = queries.shape[1] // HEAD_SIZE
    kv_here = keys.shape[1] // HEAD_SIZE
    group_width = QUERY_HEADS // KEY_VALUE_HEADS
    cycle_size = lax.axis_size("ctx")
    section_size, tp_size = lax.axis_size("section"), lax.axis_size("tp")
    tp_index = lax.axis_index("tp")
    local_kv = tp_index * heads_here // group_width
    group = (
        lax.axis_index("section") * tp_size + tp_index,
        section_size * tp_size,
        tp_size,
    )
    core, across, near, far = tp_size, 2 * tp_size, 1, 2
    orders = {False: (core, across, near, far), True: (core, near, far, across)}

    pair = jnp.stack(
        [
            lax.dynamic_slice_in_dim(keys, local_kv * HEAD_SIZE, HEAD_SIZE, 1),
            lax.dynamic_slice_in_dim(values, local_kv * HEAD_SIZE, HEAD_SIZE, 1),
        ]
    )
    pairs = [pair] + [shifted(pair, "ctx", -turn) for turn in range(1, cycle_size)]
    scored_grad = from_last(out_grad, "ctx", pairs[1:])
    latents = enc_weight.shape[1] // group[1]
    weights = {"dec": dec_weight, "enc": enc_weight}
    full = max(first + width for _, first, width, *_ in SCHEDULE)
    schedule, unit = (SHORT_SCHEDULE, latents) if latents % full else (SCHEDULE, latents // full)
    chunks = [
        Chunk(kind, first * unit, width * unit, times, orders[late])
        for kind, first, width, times, late in schedule
    ]
    steps = [
        [(chunk, chunk.steps.index(step)) for chunk in chunks if step in chunk.steps]
        for step in range(1 + max(chunk.steps[-1] for chunk in chunks))
    ]
    acts = {"dec": scored_grad}
    early = next(step for step, jobs in enumerate(steps) if any(c.kind == "enc" for c, _ in jobs))
    run_step(steps[0], acts, weights, group[1], latents, tp_size, None)
    queries, _ = lax.optimization_barrier((queries, acts["dec"]))
    attn_flat, query_grad, *terms = pl.pallas_call(
        functools.partial(attention_kernel, cycle_size),
        out_shape=[
            jax.ShapeDtypeStruct(queries.shape, jnp.bfloat16),
            jax.ShapeDtypeStruct(queries.shape, jnp.bfloat16),
            *[jax.ShapeDtypeStruct(pair.shape, jnp.float32)] * cycle_size,
        ],
        compiler_params=pltpu.CompilerParams(vmem_limit_bytes=32 * 2**20),
    )(queries, out_grad, *pairs)
    acts["dec"], _ = lax.optimization_barrier((acts["dec"], attn_flat))
    for step in range(1, early):
        run_step(steps[step], acts, weights, group[1], latents, tp_size, None)
    scored_out = from_last(attn_flat, "ctx", (acts["dec"],))
    wide_out = scored_out.astype(jnp.float32)
    squares = jnp.sum(wide_out * wide_out, axis=1)
    acts["enc"], _ = lax.optimization_barrier((scored_out, acts["dec"]))

    def add_squares(axis, mask, token):
        nonlocal squares
        other = swapped(squares, axis, mask)
        squares, _ = lax.optimization_barrier((squares, token))
        squares = squares + other

    def gather_blocks(token):
        nonlocal summed
        others = [shifted(terms[turn], "ctx", turn) for turn in range(1, cycle_size)]
        summed, _ = lax.optimization_barrier((terms[0], token))
        for other in others:
            summed = summed + other

    def add_heads(mask, token):
        nonlocal summed
        other = swapped(summed, "tp", mask)
        summed, _ = lax.optimization_barrier((summed, token))
        summed = summed + other

    def gather_heads(token):
        nonlocal summed
        half = summed.astype(jnp.bfloat16)
        others = [swapped(half, "tp", share * step) for step in range(1, kv_here)]
        half, _ = lax.optimization_barrier((half, token))
        slots, columns = [half, *others], []
        for column in range(kv_here):
            value = slots[0]
            for step in range(1, kv_here):
                value = jnp.where((local_kv ^ step) == column, slots[step], value)
            columns.append(value)
        summed = jnp.concatenate(columns, axis=2)

    summed = terms[0]
    share = group_width // heads_here
    bits = lambda count: [1 << i for i in range((count - 1).bit_length())]
    tasks = {}
    square_tasks = [functools.partial(add_squares, "section", m) for m in bits(section_size)]
    square_tasks += [functools.partial(add_squares, "tp", m) for m in bits(tp_size)]
    term_tasks = [gather_blocks]
    term_tasks += [functools.partial(add_heads, mask) for mask in bits(share)]
    term_tasks += [gather_heads]
    for first, items in ((FIRST_SQUARES, square_tasks), (FIRST_TERMS, term_tasks)):
        for number, item in enumerate(items):
            tasks.setdefault(first + number, []).append(item)

    bias = enc_bias.reshape(1, latents)

    def finish(chunk):
        end = chunk.offset + chunk.width
        inverse = jnp.broadcast_to(
            lax.rsqrt(squares / D_Z + 1e-06)[:, None], (row_count, HEAD_SIZE)
        )
        values, pieces = [inverse, bias], []
        for other in chunks:
            first, last = max(other.offset, chunk.offset), min(other.offset + other.width, end)
            if other.kind == "dec" and first < last:
                values.append(other.result)
                pieces.append((first - other.offset, last - other.offset))
        return values, pieces

    for step, jobs in enumerate(steps[early:], early):
        run_step(jobs, acts, weights, group[1], latents, tp_size, finish)
        for task in tasks.get(step, ()):
            task(acts["enc"])
        if step in tasks:
            acts["enc"], _, _ = lax.optimization_barrier((acts["enc"], squares, summed))
    scores = sorted((c for c in chunks if c.kind == "enc"), key=lambda c: c.offset)
    feature_scores = jnp.concatenate([c.result[0] for c in scores], axis=1).reshape(latents)
    return (query_grad, summed[0], summed[1], feature_scores)


def solution(mesh):
    placed = (
        P("ctx", ("section", "tp")),
        P("ctx", "section"),
        P("ctx", "section"),
        P("ctx", ("section", "tp")),
        P(("section", "tp"), "ctx"),
        P(("ctx", "section", "tp")),
        P("ctx", ("section", "tp")),
    )
    return jax.shard_map(
        body,
        mesh=mesh,
        in_specs=placed,
        out_specs=(
            P("ctx", ("section", "tp")),
            P("ctx", "section"),
            P("ctx", "section"),
            P(("ctx", "section", "tp")),
        ),
        check_vma=False,
    )
```

```python
import functools
import math

import jax
import jax.numpy as jnp
from jax import lax
from jax.experimental import pallas as pl
from jax.experimental.pallas import tpu as pltpu
from jax.sharding import PartitionSpec as P

QUERY_HEADS = 64
KEY_VALUE_HEADS = 8
HEAD_SIZE = 128
D_Z = 8192

SCHEDULE = (
    ("dec", 0, 512, (0, 1, 3, 5, 7), False),
    ("dec", 512, 512, (0, 2, 4, 6, 8), True),
    ("dec", 1024, 1024, (1, 3, 5, 7, 9), False),
    ("enc", 1280, 768, (2, 4, 6, 8, 10), False),
    ("enc", 768, 512, (3, 5, 7, 9, 11), False),
    ("enc", 256, 512, (4, 6, 8, 10, 12), False),
    ("enc", 0, 256, (5, 7, 9, 10, 12), False),
)
SHORT_SCHEDULE = (
    ("dec", 0, 1, (0, 2, 4, 6, 8), False),
    ("enc", 0, 1, (1, 3, 5, 7, 9), False),
)
COST = 100
AHEAD = 16
TOGETHER = 4096
FIRST_SQUARES = 4
FIRST_TERMS = 3


def shifted(value, axis, steps):
    count = lax.axis_size(axis)
    return lax.ppermute(value, axis, [(i, (i + steps) % count) for i in range(count)])


def swapped(value, axis, mask):
    count = lax.axis_size(axis)
    return lax.ppermute(value, axis, [(i, i ^ mask) for i in range(count)])


def from_last(value, axis, tokens=()):
    count = lax.axis_size(axis)
    rank = count - 1 - lax.axis_index(axis)
    reach = 1
    while reach < count:
        pairs = [
            (count - 1 - i, count - 1 - i - reach) for i in range(reach) if i + reach < count
        ]
        moved = lax.ppermute(value, axis, pairs)
        value, *_ = lax.optimization_barrier((value, *tokens))
        tokens = ()
        value = jnp.where((rank >= reach) & (rank < 2 * reach), moved, value)
        reach *= 2
    return value


def attention_kernel(cycle_size, queries, out_grad, *refs):
    pairs, (attn, query_grad, *terms) = refs[:cycle_size], refs[cycle_size:]
    rows, columns = queries.shape
    half = rows // 2
    scale = 1.0 / math.sqrt(HEAD_SIZE)
    me = lax.axis_index("ctx")

    def positions(device, axis):
        local = lax.broadcasted_iota(jnp.int32, (rows, rows), axis)
        late = (2 * cycle_size - 1 - device) * half + local - half
        return jnp.where(local >= half, late, device * half + local)

    mine = positions(me, 0)
    causal = jnp.concatenate(
        [
            (mine - positions(lax.rem(me + turn, cycle_size), 1)).astype(jnp.float32)
            for turn in range(cycle_size)
        ],
        axis=1,
    ) >= 0.0
    keys = jnp.concatenate([ref[0] for ref in pairs], axis=0)
    values = jnp.concatenate([ref[1] for ref in pairs], axis=0)
    key_term = value_term = 0.0

    def dot(left, right, left_dim, right_dim):
        return lax.dot_general(
            left, right, (((left_dim,), (right_dim,)), ((), ())),
            preferred_element_type=jnp.float32,
        )

    for first in range(0, columns, HEAD_SIZE):
        head = slice(first, first + HEAD_SIZE)
        query, grad = queries[:, head], out_grad[:, head]
        logits = jnp.where(causal, dot(query, keys, 1, 1) * scale, -1e30)
        raised = jnp.where(causal, jnp.exp(logits - jnp.max(logits, axis=1, keepdims=True)), 0.0)
        weights = raised / jnp.sum(raised, axis=1, keepdims=True)
        high = weights.astype(jnp.bfloat16)
        low = (weights - high.astype(jnp.float32)).astype(jnp.bfloat16)
        out = (dot(high, values, 1, 0) + dot(low, values, 1, 0)).astype(jnp.bfloat16)
        attn[:, head] = out
        row_dots = jnp.sum(
            grad.astype(jnp.float32) * out.astype(jnp.float32), axis=1, keepdims=True
        )
        value_term += dot(high, grad, 0, 0)
        logit_half = (weights * (dot(grad, values, 1, 1) - row_dots)).astype(jnp.bfloat16)
        query_grad[:, head] = (dot(logit_half, keys, 1, 0) * scale).astype(jnp.bfloat16)
        key_term += dot(logit_half, query, 0, 0)
    for turn, ref in enumerate(terms):
        block = slice(turn * rows, (turn + 1) * rows)
        ref[0] = key_term[block] * scale
        ref[1] = value_term[block]


def relative_blocks(order, stage, size):
    done = sum(order[:stage])
    bit = order[stage] if stage < len(order) else 0
    return [r for r in range(size) if not r & done and (r & bit or r == bit)]


class Chunk:
    def __init__(self, kind, offset, width, steps, order):
        self.kind, self.offset, self.width, self.order = kind, offset, width, order
        self.steps = steps
        self.received = []
        self.result = None


def step_kernel(plan, size, latents, tp, *refs):
    refs = list(refs)
    take = lambda count: [refs.pop(0) for _ in range(count)]
    kinds, jobs, pieces = plan["kinds"], plan["jobs"], plan["pieces"]
    sources = {kind: take(2) for kind in kinds}
    incoming = [take(stage) for _, stage in jobs]
    extras = [take(2 + len(piece)) if piece else () for piece in pieces]
    outs = take(len(jobs))
    acts = {kind: take(1)[0] for kind in kinds}
    weight_bufs, sum_bufs, out_bufs, extra_bufs = [], [], [], []
    for (_, stage), piece in zip(jobs, pieces):
        weight_bufs.append(take(1)[0])
        sum_bufs.append(take(stage))
        out_bufs.append(take(1)[0])
        extra_bufs.append(take(3) if piece else ())
    sems = take(1)[0]
    me = lax.axis_index("section") * tp + lax.axis_index("tp")
    used = 0

    def copy(source, target):
        nonlocal used
        used += 1
        return pltpu.make_async_copy(source, target, sems.at[used - 1])

    arrivals, seen = [], set()
    for number, (chunk, stage) in enumerate(jobs):
        blocks = relative_blocks(chunk.order, stage, size)
        weight = sources[chunk.kind][1]
        for index, r in enumerate(blocks):
            first = pl.multiple_of((me ^ r) * latents + chunk.offset, 128)
            if chunk.kind == "dec":
                piece = weight.at[pl.ds(first, chunk.width), :]
            else:
                piece = weight.at[:, pl.ds(first, chunk.width)]
            wanted = [copy(piece, weight_bufs[number].at[index])]
            if chunk.kind not in seen:
                seen.add(chunk.kind)
                wanted.insert(0, copy(sources[chunk.kind][0], acts[chunk.kind]))
            for earlier in range(stage):
                for place, to, count in runs(chunk.order, earlier, stage, size):
                    if to == index:
                        source = incoming[number][earlier].at[pl.ds(place, count)]
                        target = sum_bufs[number][earlier].at[pl.ds(to, count)]
                        wanted.append(copy(source, target))
            if pieces[number]:
                inverse, bias, *attribs = extras[number]
                inverse_buf, bias_buf, attrib_buf = extra_bufs[number]
                wanted.append(copy(inverse, inverse_buf))
                wanted.append(copy(bias.at[:, pl.ds(chunk.offset, chunk.width)], bias_buf))
                place = 0
                for ref, (first, last) in zip(attribs, pieces[number]):
                    source = ref.at[0, :, pl.ds(first, last - first)]
                    wanted.append(copy(source, attrib_buf.at[:, pl.ds(place, last - first)]))
                    place += last - first
            arrivals.append(wanted)
    for item in sum(arrivals[:AHEAD], []):
        item.start()
    leaving, current = [], 0
    for number, (chunk, stage) in enumerate(jobs):
        act = acts[chunk.kind]
        count, sent = len(relative_blocks(chunk.order, stage, size)), 0
        for index in range(count):
            for item in arrivals[current]:
                item.wait()
            for item in sum(arrivals[current + AHEAD : current + AHEAD + 1], []):
                item.start()
            current += 1
            total = lax.dot_general(
                act[...],
                weight_bufs[number][index],
                (((1,), (1 if chunk.kind == "dec" else 0,)), ((), ())),
                preferred_element_type=jnp.float32,
            )
            for buf in sum_bufs[number]:
                total = total + buf[index].astype(jnp.float32)
            if pieces[number]:
                inverse_buf, bias_buf, attrib_buf = extra_bufs[number]
                active = jnp.maximum(total * inverse_buf[:, :1] + bias_buf[...], 0.0)
                total = jnp.sum(active * attrib_buf[...], axis=0, keepdims=True)
            out_bufs[number][index] = total.astype(out_bufs[number].dtype)
            if index + 1 == count or (index + 1 - sent) * chunk.width >= TOGETHER:
                part = pl.ds(sent, index + 1 - sent)
                item = copy(out_bufs[number].at[part], outs[number].at[part])
                item.start()
                leaving.append(item)
                sent = index + 1
    for item in leaving:
        item.wait()


def runs(order, earlier, stage, size):
    sent = relative_blocks(order, earlier, size)
    found = []
    for index, r in enumerate(relative_blocks(order, stage, size)):
        place = sent.index(r ^ order[earlier])
        if found and found[-1][0] + found[-1][2] == place:
            found[-1][2] += 1
        else:
            found.append([place, index, 1])
    return found


def run_step(jobs, acts, weights, size, latents, tp, finish):
    kinds = [kind for kind in ("dec", "enc") if any(c.kind == kind for c, _ in jobs)]
    rows, inner = acts[kinds[0]].shape
    operands = []
    anywhere = pl.BlockSpec(memory_space=pltpu.HBM)
    for kind in kinds:
        operands += [acts[kind], weights[kind]]
    for chunk, stage in jobs:
        operands += chunk.received[:stage]
    scratch = [pltpu.VMEM((rows, inner), jnp.bfloat16)] * len(kinds)
    outs, pieces, copies, flops, moved = [], [], len(kinds), 0, 0
    for chunk, stage in jobs:
        last = stage == len(chunk.order)
        count = len(relative_blocks(chunk.order, stage, size))
        shape = (count, rows, chunk.width)
        dtype = jnp.float32 if last else jnp.bfloat16
        pieces.append(())
        side = (chunk.width, inner) if chunk.kind == "dec" else (inner, chunk.width)
        scratch.append(pltpu.VMEM((count, *side), jnp.bfloat16))
        scratch += [pltpu.VMEM(shape, jnp.bfloat16)] * stage
        if last and chunk.kind == "enc":
            values, pieces[-1] = finish(chunk)
            operands += values
            copies += len(values)
            shape = (1, 1, chunk.width)
        scratch.append(pltpu.VMEM(shape, dtype))
        if pieces[-1]:
            scratch += [
                pltpu.VMEM((rows, HEAD_SIZE), jnp.float32),
                pltpu.VMEM((1, chunk.width), jnp.float32),
                pltpu.VMEM((rows, chunk.width), jnp.float32),
            ]
        outs.append(jax.ShapeDtypeStruct(shape, dtype))
        copies += count * (stage + 2)
        flops += 2 * count * rows * inner * chunk.width
        moved += 2 * count * chunk.width * (inner + (stage + 1) * rows)
    results = pl.pallas_call(
        functools.partial(
            step_kernel, {"kinds": kinds, "jobs": jobs, "pieces": pieces}, size, latents, tp
        ),
        out_shape=outs,
        in_specs=[anywhere] * len(operands),
        out_specs=[anywhere] * len(outs),
        scratch_shapes=[*scratch, pltpu.SemaphoreType.DMA((copies,))],
        compiler_params=pltpu.CompilerParams(vmem_limit_bytes=32 * 2**20),
        cost_estimate=pl.CostEstimate(
            flops=int(COST * flops), bytes_accessed=int(COST * moved), transcendentals=0
        ),
    )(*operands)
    for kind in acts:
        acts[kind], _ = lax.optimization_barrier((acts[kind], results[0]))
    for (chunk, stage), value in zip(jobs, results):
        chunk.latest = value
        if stage == len(chunk.order):
            chunk.result = value
        elif chunk.order[stage] >= tp:
            chunk.received.append(swapped(value, "section", chunk.order[stage] // tp))
        else:
            chunk.received.append(swapped(value, "tp", chunk.order[stage]))


def body(queries, keys, values, out_grad, enc_weight, enc_bias, dec_weight):
    row_count = queries.shape[0]
    heads_here = queries.shape[1] // HEAD_SIZE
    kv_here = keys.shape[1] // HEAD_SIZE
    group_width = QUERY_HEADS // KEY_VALUE_HEADS
    cycle_size = lax.axis_size("ctx")
    section_size, tp_size = lax.axis_size("section"), lax.axis_size("tp")
    tp_index = lax.axis_index("tp")
    local_kv = tp_index * heads_here // group_width
    group = (
        lax.axis_index("section") * tp_size + tp_index,
        section_size * tp_size,
        tp_size,
    )
    core, across, near, far = tp_size, 2 * tp_size, 1, 2
    orders = {False: (core, across, near, far), True: (core, near, far, across)}

    pair = jnp.stack(
        [
            lax.dynamic_slice_in_dim(keys, local_kv * HEAD_SIZE, HEAD_SIZE, 1),
            lax.dynamic_slice_in_dim(values, local_kv * HEAD_SIZE, HEAD_SIZE, 1),
        ]
    )
    pairs = [pair] + [shifted(pair, "ctx", -turn) for turn in range(1, cycle_size)]
    scored_grad = from_last(out_grad, "ctx", pairs[1:])
    latents = enc_weight.shape[1] // group[1]
    weights = {"dec": dec_weight, "enc": enc_weight}
    full = max(first + width for _, first, width, *_ in SCHEDULE)
    schedule, unit = (SHORT_SCHEDULE, latents) if latents % full else (SCHEDULE, latents // full)
    chunks = [
        Chunk(kind, first * unit, width * unit, times, orders[late])
        for kind, first, width, times, late in schedule
    ]
    steps = [
        [(chunk, chunk.steps.index(step)) for chunk in chunks if step in chunk.steps]
        for step in range(1 + max(chunk.steps[-1] for chunk in chunks))
    ]
    acts = {"dec": scored_grad}
    early = next(step for step, jobs in enumerate(steps) if any(c.kind == "enc" for c, _ in jobs))
    run_step(steps[0], acts, weights, group[1], latents, tp_size, None)
    queries, _ = lax.optimization_barrier((queries, acts["dec"]))
    attn_flat, query_grad, *terms = pl.pallas_call(
        functools.partial(attention_kernel, cycle_size),
        out_shape=[
            jax.ShapeDtypeStruct(queries.shape, jnp.bfloat16),
            jax.ShapeDtypeStruct(queries.shape, jnp.bfloat16),
            *[jax.ShapeDtypeStruct(pair.shape, jnp.float32)] * cycle_size,
        ],
        compiler_params=pltpu.CompilerParams(vmem_limit_bytes=32 * 2**20),
    )(queries, out_grad, *pairs)
    acts["dec"], _ = lax.optimization_barrier((acts["dec"], attn_flat))
    for step in range(1, early):
        run_step(steps[step], acts, weights, group[1], latents, tp_size, None)
    scored_out = from_last(attn_flat, "ctx", (acts["dec"],))
    wide_out = scored_out.astype(jnp.float32)
    squares = jnp.sum(wide_out * wide_out, axis=1)
    acts["enc"], _ = lax.optimization_barrier((scored_out, acts["dec"]))

    def add_squares(axis, mask, token):
        nonlocal squares
        other = swapped(squares, axis, mask)
        squares, _ = lax.optimization_barrier((squares, token))
        squares = squares + other

    def gather_blocks(token):
        nonlocal summed
        others = [shifted(terms[turn], "ctx", turn) for turn in range(1, cycle_size)]
        summed, _ = lax.optimization_barrier((terms[0], token))
        for other in others:
            summed = summed + other

    def add_heads(mask, token):
        nonlocal summed
        other = swapped(summed, "tp", mask)
        summed, _ = lax.optimization_barrier((summed, token))
        summed = summed + other

    def gather_heads(token):
        nonlocal summed
        half = summed.astype(jnp.bfloat16)
        others = [swapped(half, "tp", share * step) for step in range(1, kv_here)]
        half, _ = lax.optimization_barrier((half, token))
        slots, columns = [half, *others], []
        for column in range(kv_here):
            value = slots[0]
            for step in range(1, kv_here):
                value = jnp.where((local_kv ^ step) == column, slots[step], value)
            columns.append(value)
        summed = jnp.concatenate(columns, axis=2)

    summed = terms[0]
    share = group_width // heads_here
    bits = lambda count: [1 << i for i in range((count - 1).bit_length())]
    tasks = {}
    square_tasks = [functools.partial(add_squares, "section", m) for m in bits(section_size)]
    square_tasks += [functools.partial(add_squares, "tp", m) for m in bits(tp_size)]
    term_tasks = [gather_blocks]
    term_tasks += [functools.partial(add_heads, mask) for mask in bits(share)]
    term_tasks += [gather_heads]
    for first, items in ((FIRST_SQUARES, square_tasks), (FIRST_TERMS, term_tasks)):
        for number, item in enumerate(items):
            tasks.setdefault(first + number, []).append(item)

    bias = enc_bias.reshape(1, latents)

    def finish(chunk):
        end = chunk.offset + chunk.width
        inverse = jnp.broadcast_to(
            lax.rsqrt(squares / D_Z + 1e-06)[:, None], (row_count, HEAD_SIZE)
        )
        values, pieces = [inverse, bias], []
        for other in chunks:
            first, last = max(other.offset, chunk.offset), min(other.offset + other.width, end)
            if other.kind == "dec" and first < last:
                values.append(other.result)
                pieces.append((first - other.offset, last - other.offset))
        return values, pieces

    for step, jobs in enumerate(steps[early:], early):
        run_step(jobs, acts, weights, group[1], latents, tp_size, finish)
        for task in tasks.get(step, ()):
            task(acts["enc"])
        if step in tasks:
            acts["enc"], _, _ = lax.optimization_barrier((acts["enc"], squares, summed))
    scores = sorted((c for c in chunks if c.kind == "enc"), key=lambda c: c.offset)
    feature_scores = jnp.concatenate([c.result[0] for c in scores], axis=1).reshape(latents)
    return (query_grad, summed[0], summed[1], feature_scores)


def solution(mesh):
    placed = (
        P("ctx", ("section", "tp")),
        P("ctx", "section"),
        P("ctx", "section"),
        P("ctx", ("section", "tp")),
        P(("section", "tp"), "ctx"),
        P(("ctx", "section", "tp")),
        P("ctx", ("section", "tp")),
    )
    return jax.shard_map(
        body,
        mesh=mesh,
        in_specs=placed,
        out_specs=(
            P("ctx", ("section", "tp")),
            P("ctx", "section"),
            P("ctx", "section"),
            P(("ctx", "section", "tp")),
        ),
        check_vma=False,
    )
```

```python
import functools
import math

import jax
import jax.numpy as jnp
from jax import lax
from jax.experimental import pallas as pl
from jax.experimental.pallas import tpu as pltpu
from jax.sharding import PartitionSpec as P

QUERY_HEADS = 64
KEY_VALUE_HEADS = 8
HEAD_SIZE = 128
D_Z = 8192

SCHEDULE = (
    ("dec", 0, 512, (0, 1, 3, 5, 7), False),
    ("dec", 512, 512, (0, 2, 4, 6, 8), True),
    ("dec", 1024, 1024, (1, 3, 5, 7, 9), False),
    ("enc", 1280, 768, (2, 4, 6, 8, 10), False),
    ("enc", 768, 512, (3, 5, 7, 9, 11), False),
    ("enc", 256, 512, (4, 6, 8, 10, 12), False),
    ("enc", 0, 256, (5, 7, 9, 10, 12), False),
)
SHORT_SCHEDULE = (
    ("dec", 0, 1, (0, 2, 4, 6, 8), False),
    ("enc", 0, 1, (1, 3, 5, 7, 9), False),
)
COST = 30
AHEAD = 16
TOGETHER = 4096
FIRST_SQUARES = 4
FIRST_TERMS = 3


def shifted(value, axis, steps):
    count = lax.axis_size(axis)
    return lax.ppermute(value, axis, [(i, (i + steps) % count) for i in range(count)])


def swapped(value, axis, mask):
    count = lax.axis_size(axis)
    return lax.ppermute(value, axis, [(i, i ^ mask) for i in range(count)])


def from_last(value, axis, tokens=()):
    count = lax.axis_size(axis)
    rank = count - 1 - lax.axis_index(axis)
    reach = 1
    while reach < count:
        pairs = [
            (count - 1 - i, count - 1 - i - reach) for i in range(reach) if i + reach < count
        ]
        moved = lax.ppermute(value, axis, pairs)
        value, *_ = lax.optimization_barrier((value, *tokens))
        tokens = ()
        value = jnp.where((rank >= reach) & (rank < 2 * reach), moved, value)
        reach *= 2
    return value


def attention_kernel(cycle_size, queries, out_grad, *refs):
    pairs, (attn, query_grad, *terms) = refs[:cycle_size], refs[cycle_size:]
    rows, columns = queries.shape
    half = rows // 2
    scale = 1.0 / math.sqrt(HEAD_SIZE)
    me = lax.axis_index("ctx")

    def positions(device, axis):
        local = lax.broadcasted_iota(jnp.int32, (rows, rows), axis)
        late = (2 * cycle_size - 1 - device) * half + local - half
        return jnp.where(local >= half, late, device * half + local)

    mine = positions(me, 0)
    causal = jnp.concatenate(
        [
            (mine - positions(lax.rem(me + turn, cycle_size), 1)).astype(jnp.float32)
            for turn in range(cycle_size)
        ],
        axis=1,
    ) >= 0.0
    keys = jnp.concatenate([ref[0] for ref in pairs], axis=0)
    values = jnp.concatenate([ref[1] for ref in pairs], axis=0)
    key_term = value_term = 0.0

    def dot(left, right, left_dim, right_dim):
        return lax.dot_general(
            left, right, (((left_dim,), (right_dim,)), ((), ())),
            preferred_element_type=jnp.float32,
        )

    for first in range(0, columns, HEAD_SIZE):
        head = slice(first, first + HEAD_SIZE)
        query, grad = queries[:, head], out_grad[:, head]
        logits = jnp.where(causal, dot(query, keys, 1, 1) * scale, -1e30)
        raised = jnp.where(causal, jnp.exp(logits - jnp.max(logits, axis=1, keepdims=True)), 0.0)
        weights = raised / jnp.sum(raised, axis=1, keepdims=True)
        high = weights.astype(jnp.bfloat16)
        low = (weights - high.astype(jnp.float32)).astype(jnp.bfloat16)
        out = (dot(high, values, 1, 0) + dot(low, values, 1, 0)).astype(jnp.bfloat16)
        attn[:, head] = out
        row_dots = jnp.sum(
            grad.astype(jnp.float32) * out.astype(jnp.float32), axis=1, keepdims=True
        )
        value_term += dot(high, grad, 0, 0)
        logit_half = (weights * (dot(grad, values, 1, 1) - row_dots)).astype(jnp.bfloat16)
        query_grad[:, head] = (dot(logit_half, keys, 1, 0) * scale).astype(jnp.bfloat16)
        key_term += dot(logit_half, query, 0, 0)
    for turn, ref in enumerate(terms):
        block = slice(turn * rows, (turn + 1) * rows)
        ref[0] = key_term[block] * scale
        ref[1] = value_term[block]


def relative_blocks(order, stage, size):
    done = sum(order[:stage])
    bit = order[stage] if stage < len(order) else 0
    return [r for r in range(size) if not r & done and (r & bit or r == bit)]


class Chunk:
    def __init__(self, kind, offset, width, steps, order):
        self.kind, self.offset, self.width, self.order = kind, offset, width, order
        self.steps = steps
        self.received = []
        self.result = None


def step_kernel(plan, size, latents, tp, *refs):
    refs = list(refs)
    take = lambda count: [refs.pop(0) for _ in range(count)]
    kinds, jobs, pieces = plan["kinds"], plan["jobs"], plan["pieces"]
    sources = {kind: take(2) for kind in kinds}
    incoming = [take(stage) for _, stage in jobs]
    extras = [take(2 + len(piece)) if piece else () for piece in pieces]
    outs = take(len(jobs))
    acts = {kind: take(1)[0] for kind in kinds}
    weight_bufs, sum_bufs, out_bufs, extra_bufs = [], [], [], []
    for (_, stage), piece in zip(jobs, pieces):
        weight_bufs.append(take(1)[0])
        sum_bufs.append(take(stage))
        out_bufs.append(take(1)[0])
        extra_bufs.append(take(3) if piece else ())
    sems = take(1)[0]
    me = lax.axis_index("section") * tp + lax.axis_index("tp")
    used = 0

    def copy(source, target):
        nonlocal used
        used += 1
        return pltpu.make_async_copy(source, target, sems.at[used - 1])

    arrivals, seen = [], set()
    for number, (chunk, stage) in enumerate(jobs):
        blocks = relative_blocks(chunk.order, stage, size)
        weight = sources[chunk.kind][1]
        for index, r in enumerate(blocks):
            first = pl.multiple_of((me ^ r) * latents + chunk.offset, 128)
            if chunk.kind == "dec":
                piece = weight.at[pl.ds(first, chunk.width), :]
            else:
                piece = weight.at[:, pl.ds(first, chunk.width)]
            wanted = [copy(piece, weight_bufs[number].at[index])]
            if chunk.kind not in seen:
                seen.add(chunk.kind)
                wanted.insert(0, copy(sources[chunk.kind][0], acts[chunk.kind]))
            for earlier in range(stage):
                for place, to, count in runs(chunk.order, earlier, stage, size):
                    if to == index:
                        source = incoming[number][earlier].at[pl.ds(place, count)]
                        target = sum_bufs[number][earlier].at[pl.ds(to, count)]
                        wanted.append(copy(source, target))
            if pieces[number]:
                inverse, bias, *attribs = extras[number]
                inverse_buf, bias_buf, attrib_buf = extra_bufs[number]
                wanted.append(copy(inverse, inverse_buf))
                wanted.append(copy(bias.at[:, pl.ds(chunk.offset, chunk.width)], bias_buf))
                place = 0
                for ref, (first, last) in zip(attribs, pieces[number]):
                    source = ref.at[0, :, pl.ds(first, last - first)]
                    wanted.append(copy(source, attrib_buf.at[:, pl.ds(place, last - first)]))
                    place += last - first
            arrivals.append(wanted)
    for item in sum(arrivals[:AHEAD], []):
        item.start()
    leaving, current = [], 0
    for number, (chunk, stage) in enumerate(jobs):
        act = acts[chunk.kind]
        count, sent = len(relative_blocks(chunk.order, stage, size)), 0
        for index in range(count):
            for item in arrivals[current]:
                item.wait()
            for item in sum(arrivals[current + AHEAD : current + AHEAD + 1], []):
                item.start()
            current += 1
            total = lax.dot_general(
                act[...],
                weight_bufs[number][index],
                (((1,), (1 if chunk.kind == "dec" else 0,)), ((), ())),
                preferred_element_type=jnp.float32,
            )
            for buf in sum_bufs[number]:
                total = total + buf[index].astype(jnp.float32)
            if pieces[number]:
                inverse_buf, bias_buf, attrib_buf = extra_bufs[number]
                active = jnp.maximum(total * inverse_buf[:, :1] + bias_buf[...], 0.0)
                total = jnp.sum(active * attrib_buf[...], axis=0, keepdims=True)
            out_bufs[number][index] = total.astype(out_bufs[number].dtype)
            if index + 1 == count or (index + 1 - sent) * chunk.width >= TOGETHER:
                part = pl.ds(sent, index + 1 - sent)
                item = copy(out_bufs[number].at[part], outs[number].at[part])
                item.start()
                leaving.append(item)
                sent = index + 1
    for item in leaving:
        item.wait()


def runs(order, earlier, stage, size):
    sent = relative_blocks(order, earlier, size)
    found = []
    for index, r in enumerate(relative_blocks(order, stage, size)):
        place = sent.index(r ^ order[earlier])
        if found and found[-1][0] + found[-1][2] == place:
            found[-1][2] += 1
        else:
            found.append([place, index, 1])
    return found


def run_step(jobs, acts, weights, size, latents, tp, finish):
    kinds = [kind for kind in ("dec", "enc") if any(c.kind == kind for c, _ in jobs)]
    rows, inner = acts[kinds[0]].shape
    operands = []
    anywhere = pl.BlockSpec(memory_space=pltpu.HBM)
    for kind in kinds:
        operands += [acts[kind], weights[kind]]
    for chunk, stage in jobs:
        operands += chunk.received[:stage]
    scratch = [pltpu.VMEM((rows, inner), jnp.bfloat16)] * len(kinds)
    outs, pieces, copies, flops, moved = [], [], len(kinds), 0, 0
    for chunk, stage in jobs:
        last = stage == len(chunk.order)
        count = len(relative_blocks(chunk.order, stage, size))
        shape = (count, rows, chunk.width)
        dtype = jnp.float32 if last else jnp.bfloat16
        pieces.append(())
        side = (chunk.width, inner) if chunk.kind == "dec" else (inner, chunk.width)
        scratch.append(pltpu.VMEM((count, *side), jnp.bfloat16))
        scratch += [pltpu.VMEM(shape, jnp.bfloat16)] * stage
        if last and chunk.kind == "enc":
            values, pieces[-1] = finish(chunk)
            operands += values
            copies += len(values)
            shape = (1, 1, chunk.width)
        scratch.append(pltpu.VMEM(shape, dtype))
        if pieces[-1]:
            scratch += [
                pltpu.VMEM((rows, HEAD_SIZE), jnp.float32),
                pltpu.VMEM((1, chunk.width), jnp.float32),
                pltpu.VMEM((rows, chunk.width), jnp.float32),
            ]
        outs.append(jax.ShapeDtypeStruct(shape, dtype))
        copies += count * (stage + 2)
        flops += 2 * count * rows * inner * chunk.width
        moved += 2 * count * chunk.width * (inner + (stage + 1) * rows)
    results = pl.pallas_call(
        functools.partial(
            step_kernel, {"kinds": kinds, "jobs": jobs, "pieces": pieces}, size, latents, tp
        ),
        out_shape=outs,
        in_specs=[anywhere] * len(operands),
        out_specs=[anywhere] * len(outs),
        scratch_shapes=[*scratch, pltpu.SemaphoreType.DMA((copies,))],
        compiler_params=pltpu.CompilerParams(vmem_limit_bytes=32 * 2**20),
        cost_estimate=pl.CostEstimate(
            flops=int(COST * flops), bytes_accessed=int(COST * moved), transcendentals=0
        ),
    )(*operands)
    for kind in acts:
        acts[kind], _ = lax.optimization_barrier((acts[kind], results[0]))
    for (chunk, stage), value in zip(jobs, results):
        chunk.latest = value
        if stage == len(chunk.order):
            chunk.result = value
        elif chunk.order[stage] >= tp:
            chunk.received.append(swapped(value, "section", chunk.order[stage] // tp))
        else:
            chunk.received.append(swapped(value, "tp", chunk.order[stage]))


def body(queries, keys, values, out_grad, enc_weight, enc_bias, dec_weight):
    row_count = queries.shape[0]
    heads_here = queries.shape[1] // HEAD_SIZE
    kv_here = keys.shape[1] // HEAD_SIZE
    group_width = QUERY_HEADS // KEY_VALUE_HEADS
    cycle_size = lax.axis_size("ctx")
    section_size, tp_size = lax.axis_size("section"), lax.axis_size("tp")
    tp_index = lax.axis_index("tp")
    local_kv = tp_index * heads_here // group_width
    group = (
        lax.axis_index("section") * tp_size + tp_index,
        section_size * tp_size,
        tp_size,
    )
    core, across, near, far = tp_size, 2 * tp_size, 1, 2
    orders = {False: (core, across, near, far), True: (core, near, far, across)}

    pair = jnp.stack(
        [
            lax.dynamic_slice_in_dim(keys, local_kv * HEAD_SIZE, HEAD_SIZE, 1),
            lax.dynamic_slice_in_dim(values, local_kv * HEAD_SIZE, HEAD_SIZE, 1),
        ]
    )
    pairs = [pair] + [shifted(pair, "ctx", -turn) for turn in range(1, cycle_size)]
    scored_grad = from_last(out_grad, "ctx", pairs[1:])
    latents = enc_weight.shape[1] // group[1]
    weights = {"dec": dec_weight, "enc": enc_weight}
    full = max(first + width for _, first, width, *_ in SCHEDULE)
    schedule, unit = (SHORT_SCHEDULE, latents) if latents % full else (SCHEDULE, latents // full)
    chunks = [
        Chunk(kind, first * unit, width * unit, times, orders[late])
        for kind, first, width, times, late in schedule
    ]
    steps = [
        [(chunk, chunk.steps.index(step)) for chunk in chunks if step in chunk.steps]
        for step in range(1 + max(chunk.steps[-1] for chunk in chunks))
    ]
    acts = {"dec": scored_grad}
    early = next(step for step, jobs in enumerate(steps) if any(c.kind == "enc" for c, _ in jobs))
    run_step(steps[0], acts, weights, group[1], latents, tp_size, None)
    queries, _ = lax.optimization_barrier((queries, acts["dec"]))
    attn_flat, query_grad, *terms = pl.pallas_call(
        functools.partial(attention_kernel, cycle_size),
        out_shape=[
            jax.ShapeDtypeStruct(queries.shape, jnp.bfloat16),
            jax.ShapeDtypeStruct(queries.shape, jnp.bfloat16),
            *[jax.ShapeDtypeStruct(pair.shape, jnp.float32)] * cycle_size,
        ],
        compiler_params=pltpu.CompilerParams(vmem_limit_bytes=32 * 2**20),
    )(queries, out_grad, *pairs)
    acts["dec"], _ = lax.optimization_barrier((acts["dec"], attn_flat))
    for step in range(1, early):
        run_step(steps[step], acts, weights, group[1], latents, tp_size, None)
    scored_out = from_last(attn_flat, "ctx", (acts["dec"],))
    wide_out = scored_out.astype(jnp.float32)
    squares = jnp.sum(wide_out * wide_out, axis=1)
    acts["enc"], _ = lax.optimization_barrier((scored_out, acts["dec"]))

    def add_squares(axis, mask, token):
        nonlocal squares
        other = swapped(squares, axis, mask)
        squares, _ = lax.optimization_barrier((squares, token))
        squares = squares + other

    def gather_blocks(token):
        nonlocal summed
        others = [shifted(terms[turn], "ctx", turn) for turn in range(1, cycle_size)]
        summed, _ = lax.optimization_barrier((terms[0], token))
        for other in others:
            summed = summed + other

    def add_heads(mask, token):
        nonlocal summed
        other = swapped(summed, "tp", mask)
        summed, _ = lax.optimization_barrier((summed, token))
        summed = summed + other

    def gather_heads(token):
        nonlocal summed
        half = summed.astype(jnp.bfloat16)
        others = [swapped(half, "tp", share * step) for step in range(1, kv_here)]
        half, _ = lax.optimization_barrier((half, token))
        slots, columns = [half, *others], []
        for column in range(kv_here):
            value = slots[0]
            for step in range(1, kv_here):
                value = jnp.where((local_kv ^ step) == column, slots[step], value)
            columns.append(value)
        summed = jnp.concatenate(columns, axis=2)

    summed = terms[0]
    share = group_width // heads_here
    bits = lambda count: [1 << i for i in range((count - 1).bit_length())]
    tasks = {}
    square_tasks = [functools.partial(add_squares, "section", m) for m in bits(section_size)]
    square_tasks += [functools.partial(add_squares, "tp", m) for m in bits(tp_size)]
    term_tasks = [gather_blocks]
    term_tasks += [functools.partial(add_heads, mask) for mask in bits(share)]
    term_tasks += [gather_heads]
    for first, items in ((FIRST_SQUARES, square_tasks), (FIRST_TERMS, term_tasks)):
        for number, item in enumerate(items):
            tasks.setdefault(first + number, []).append(item)

    bias = enc_bias.reshape(1, latents)

    def finish(chunk):
        end = chunk.offset + chunk.width
        inverse = jnp.broadcast_to(
            lax.rsqrt(squares / D_Z + 1e-06)[:, None], (row_count, HEAD_SIZE)
        )
        values, pieces = [inverse, bias], []
        for other in chunks:
            first, last = max(other.offset, chunk.offset), min(other.offset + other.width, end)
            if other.kind == "dec" and first < last:
                values.append(other.result)
                pieces.append((first - other.offset, last - other.offset))
        return values, pieces

    for step, jobs in enumerate(steps[early:], early):
        run_step(jobs, acts, weights, group[1], latents, tp_size, finish)
        for task in tasks.get(step, ()):
            task(acts["enc"])
        if step in tasks:
            acts["enc"], _, _ = lax.optimization_barrier((acts["enc"], squares, summed))
    scores = sorted((c for c in chunks if c.kind == "enc"), key=lambda c: c.offset)
    feature_scores = jnp.concatenate([c.result[0] for c in scores], axis=1).reshape(latents)
    return (query_grad, summed[0], summed[1], feature_scores)


def solution(mesh):
    placed = (
        P("ctx", ("section", "tp")),
        P("ctx", "section"),
        P("ctx", "section"),
        P("ctx", ("section", "tp")),
        P(("section", "tp"), "ctx"),
        P(("ctx", "section", "tp")),
        P("ctx", ("section", "tp")),
    )
    return jax.shard_map(
        body,
        mesh=mesh,
        in_specs=placed,
        out_specs=(
            P("ctx", ("section", "tp")),
            P("ctx", "section"),
            P("ctx", "section"),
            P(("ctx", "section", "tp")),
        ),
        check_vma=False,
    )
```
